768 devices in a mesh: outer: 8 (over y), rep: 12 (over z_hi, x), mp: 8 (over z_lo, core).
Axes of the slice: x: 4, y: 8, z: 12 (z_hi: 3, z_lo: 4; z = z_hi * 4 + z_lo), core: 2. Of those that a mesh axis runs over, the one named last changes fastest.
Arguments:
- deltas: bfloat16 [8, 12, 768, 14336], P('outer', 'rep', None, 'mp'), may hold values from -6 to 6
- pod_momentum: float32 [8, 768, 14336], P('outer', 'rep', 'mp'), may hold values from -6 to 6
- global_momentum: float32 [12, 64, 14336], P('rep', 'outer', 'mp'), may hold values from -6 to 6
- master: float32 [12, 64, 14336], P('rep', 'outer', 'mp'), may hold values from -6 to 6
Outputs:
- params_new: bfloat16 [768, 14336], P(None, 'mp')
- pod_momentum_new: float32 [8, 768, 14336], P('outer', 'rep', 'mp')
- global_momentum_new: float32 [12, 64, 14336], P('rep', 'outer', 'mp')
The draws below stay inside these ranges and needn't reach their ends.
All inputs are finite; a program needn't handle non-finite values.
Results may differ from the reference program's by a relative error of at most 0.011.
Values may be sent and summed in bfloat16 or wider, within the bound.
No kernel may reach another device: no remote copies, remote signals or barrier semaphores. Data moves between devices by JAX's collectives and lax.ppermute only.
A program may use at most 32 MiB of HBM per device.

```python
import jax
import jax.numpy as jnp
from jax import lax

FF = 14336
ROW_DEV = 64
PODS = 8
REPLICAS = 12
ROWS = 768
N_OUTER = 8
N_REP = 12


def spiked(array, rng, source, target, blocks, factor):
    owner, partner = [(jnp.arange(array.shape[position]) // (array.shape[position] // blocks)).reshape([-1 if axis == position else 1 for axis in range(array.ndim)]) for position in (source, target)]
    chosen = jax.random.permutation(rng, blocks)[partner]
    strong = (owner == chosen) | (owner == (partner + blocks // 2) % blocks)
    return jnp.where(strong, factor * array, array)


def block_levels(stream_key, dims, split, smallest, top_value):
    level = 1.0
    for dim, parts in split:
        draws = jax.random.uniform(jax.random.fold_in(jax.random.fold_in(stream_key, 6), dim), (parts,), jnp.float32, smallest / len(split), top_value / len(split))
        level = level * jnp.repeat(jnp.exp(draws), dims[dim] // parts).reshape((-1,) + (1,) * (len(dims) - 1 - dim))
    return level


def gaussian(own_key, extent, deviation, most, shards=(), held_as=jnp.bfloat16):
    array = jax.random.normal(own_key, extent, jnp.float32) * deviation
    if len(shards) > 0:
        array = block_levels(own_key, extent, shards, -0.22, 0.18) * array
    return jnp.clip(array, min=-most, max=most).astype(held_as)


def bell_draw_with(rng, shape, scale, reach, shards, heavy, kind=jnp.bfloat16):
    result = scale * jax.random.normal(rng, shape, jnp.float32)
    if shards:
        result = result * block_levels(rng, shape, shards, -0.22, 0.18)
    return jnp.clip(spiked(result, jax.random.fold_in(rng, 3), *heavy), -reach, reach).astype(kind)


def setup_inputs(seed: int = 0) -> dict:
    keys = jax.random.split(jax.random.key(seed), 5)
    deltas = bell_draw_with(keys[0], (PODS, REPLICAS, ROWS, FF), 1.0, 6.0, ((0, 8), (1, 12), (3, 8)), (1, 2, 12, 2.0))
    pod_momentum = gaussian(keys[1], (PODS, ROWS, FF), 1.0, 6.0, ((0, 8), (1, 12), (2, 8)), jnp.float32)
    global_momentum = gaussian(keys[2], (REPLICAS, ROW_DEV, FF), 1.0, 6.0, ((0, 12), (1, 8), (2, 8)), jnp.float32)
    master = gaussian(keys[3], (REPLICAS, ROW_DEV, FF), 1.0, 6.0, ((0, 12), (1, 8), (2, 8)), jnp.float32)
    return {"deltas": deltas, "pod_momentum": pod_momentum, "global_momentum": global_momentum, "master": master}


def reference(deltas, pod_momentum, global_momentum, master):
    def one_pod(pair):
        pod_deltas, momentum = pair
        avg_delta = jnp.sum(pod_deltas.astype(jnp.float32), axis=0) / N_REP
        momentum_new = 0.9 * momentum + avg_delta
        return momentum_new, avg_delta + 0.9 * momentum_new

    pod_new, pod_update = lax.map(one_pod, (deltas, pod_momentum))
    global_mean = jnp.sum(pod_update, axis=0) / N_OUTER
    glob_old = global_momentum.reshape(ROWS, FF)
    glob_new = 0.8 * glob_old + global_mean
    params_new = (master.reshape(ROWS, FF) - 0.7 * (global_mean + 0.8 * glob_new)).astype(jnp.bfloat16)
    return params_new, pod_new, glob_new.reshape(N_REP, ROW_DEV, FF)
```

```python
import jax
import jax.numpy as jnp
from jax import lax
from jax.sharding import Mesh
from jax.sharding import PartitionSpec as P

REP = ("rep_0", "rep_1")


def exchange(blocks, axis):
    return lax.all_to_all(blocks, axis, 0, 0, tiled=True)


def total(blocks):
    return jnp.sum(blocks.astype(jnp.float32), axis=0)


def gathered(x, axis):
    return exchange(jnp.broadcast_to(x[None], (lax.axis_size(axis), *x.shape)), axis)


def shards(deltas, pod_momentum, global_momentum, master):
    n0, n1 = (lax.axis_size(a) for a in REP)
    pods = lax.axis_size("outer")
    replicas = n0 * n1
    columns = deltas.shape[-1]
    own = deltas[0, 0].reshape(n0, n1, -1, columns)
    by_x = exchange(jnp.swapaxes(own, 0, 1), "rep_1")
    by_z = exchange(total(by_x).astype(jnp.bfloat16), "rep_0")
    pod_mean = total(by_z) / replicas
    pod_new = 0.9 * pod_momentum[0] + pod_mean
    pod_update = (pod_mean + 0.9 * pod_new).astype(jnp.bfloat16)
    by_y = exchange(pod_update.reshape(pods, -1, columns), "outer")
    glob_mean = total(by_y) / pods
    glob_new = 0.8 * global_momentum[0] + glob_mean
    fresh = (master[0] - 0.7 * (glob_mean + 0.8 * glob_new)).astype(jnp.bfloat16)
    rows = gathered(gathered(fresh, "rep_0"), "outer")
    rows = gathered(jnp.swapaxes(rows, 0, 1), "rep_1")
    rows = jnp.swapaxes(rows, 0, 1).reshape(-1, columns)
    return (rows, pod_new[None], glob_new[None])


def solution(mesh):
    finer = Mesh(
        mesh.devices.reshape(mesh.shape["outer"], 3, 4, mesh.shape["mp"]),
        ("outer", "rep_0", "rep_1", "mp"),
    )
    return jax.shard_map(
        shards,
        mesh=finer,
        in_specs=(
            P("outer", REP, None, "mp"),
            P("outer", REP, "mp"),
            P(REP, "outer", "mp"),
            P(REP, "outer", "mp"),
        ),
        out_specs=(P(None, "mp"), P("outer", REP, "mp"), P(REP, "outer", "mp")),
        check_vma=False,
    )
```

```python
import jax
import jax.numpy as jnp
from jax import lax
from jax.sharding import Mesh
from jax.sharding import PartitionSpec as P

REP = ("rep_0", "rep_1")
SHARES = (4, 3)


def low(k):
    return k ^ 1


def high(k):
    return 3 - k


ROUTES = ((low, high), (high, low))


def hop(x, partner):
    return lax.ppermute(x, "rep_1", [(k, partner(k)) for k in range(4)])


def turn(x, step):
    return lax.ppermute(x, "rep_0", [(k, (k + step) % 3) for k in range(3)])


def wide(x):
    return x.astype(jnp.float32)


def narrow(x):
    return x.astype(jnp.bfloat16)


def pick(x, k, dim):
    return lax.dynamic_index_in_dim(x, k, dim, keepdims=False)


def block(own, k, h, start, width):
    n, _, rows, _ = own.shape
    half = rows // 2
    return lax.dynamic_slice(own, (0, k, h * half, start), (n, 1, half, width))[:, 0]


def first_hops(own, m, start, width):
    arrived = []
    for h, (one, two) in enumerate(ROUTES):
        sent = [block(own, k, h, start, width) for k in (one(m), two(one(m)))]
        arrived.append(hop(jnp.stack(sent), one))
    return arrived


def second_hops(own, arrived, m, start, width):
    parts = []
    for h, (one, two) in enumerate(ROUTES):
        got = arrived[h]
        onward = wide(block(own, two(m), h, start, width)) + wide(got[1])
        last = hop(narrow(onward), two)
        kept = wide(block(own, m, h, start, width)) + wide(got[0])
        parts.append(kept + wide(last))
    return jnp.concatenate(parts, axis=1)


def z_sum(parts, q):
    sent = narrow(parts)
    up = turn(pick(sent, (q + 1) % 3, 0), 1)
    down = turn(pick(sent, (q + 2) % 3, 0), 2)
    return pick(parts, q, 0) + wide(up) + wide(down)


def y_sum(update, pods):
    blocks = narrow(update).reshape(pods, -1, update.shape[-1])
    blocks = lax.all_to_all(blocks, "outer", 0, 0, tiled=True)
    return jnp.sum(wide(blocks), axis=0)


def zy_gather(fresh, pods):
    copies = jnp.broadcast_to(fresh[None], (3 * pods, *fresh.shape))
    blocks = lax.all_to_all(copies, ("rep_0", "outer"), 0, 0, tiled=True)
    return blocks.reshape(3, -1, fresh.shape[-1])


def x_gather(out, rows, m, start):
    half = rows.shape[1] // 2
    near, far = hop(rows, low), hop(rows, high)
    front = hop(far[:, :half], low)
    back = hop(near[:, half:], high)
    pieces = (
        (rows, m, 0),
        (near, low(m), 0),
        (far, high(m), 0),
        (front, low(high(m)), 0),
        (back, low(high(m)), half),
    )
    for piece, k, row in pieces:
        out = lax.dynamic_update_slice(out, piece[:, None], (0, k, row, start))
    return out


def shards(deltas, pod_momentum, global_momentum, master):
    m, q = lax.axis_index("rep_1"), lax.axis_index("rep_0")
    pods = lax.axis_size("outer")
    replicas = lax.axis_size("rep_0") * lax.axis_size("rep_1")
    columns = deltas.shape[-1]
    unit = columns // sum(SHARES)
    own = deltas[0, 0].reshape(3, 4, -1, columns)
    cuts = [(unit * sum(SHARES[:k]), unit * n) for k, n in enumerate(SHARES)]
    arrived = [first_hops(own, m, *cut) for cut in cuts]
    parts = [second_hops(own, a, m, *c) for a, c in zip(arrived, cuts, strict=True)]
    means = [z_sum(p, q) / replicas for p in parts]
    mean = jnp.concatenate(means, axis=1)
    pod_new = 0.9 * pod_momentum[0] + mean
    glob_mean = y_sum(mean + 0.9 * pod_new, pods) / pods
    glob_new = 0.8 * global_momentum[0] + glob_mean
    fresh = narrow(master[0] - 0.7 * (glob_mean + 0.8 * glob_new))
    out = jnp.zeros(own.shape, jnp.bfloat16)
    rows = []
    for start, width in cuts:
        piece = fresh[:, start : start + width]
        if rows:
            piece, rows[-1] = lax.optimization_barrier((piece, rows[-1]))
        rows.append(zy_gather(piece, pods))
    for r, (start, _) in zip(rows, cuts, strict=True):
        out = x_gather(out, r, m, start)
    return (out.reshape(-1, columns), pod_new[None], glob_new[None])


def solution(mesh):
    finer = Mesh(
        mesh.devices.reshape(mesh.shape["outer"], 3, 4, mesh.shape["mp"]),
        ("outer", "rep_0", "rep_1", "mp"),
    )
    return jax.shard_map(
        shards,
        mesh=finer,
        in_specs=(
            P("outer", REP, None, "mp"),
            P("outer", REP, "mp"),
            P(REP, "outer", "mp"),
            P(REP, "outer", "mp"),
        ),
        out_specs=(P(None, "mp"), P("outer", REP, "mp"), P(REP, "outer", "mp")),
        check_vma=False,
    )
```

```python
import jax
import jax.numpy as jnp
from jax import lax
from jax.sharding import Mesh
from jax.sharding import PartitionSpec as P

REP = ("rep_0", "rep_1")
ZY = ("rep_0", "outer")


def wide(x):
    return x.astype(jnp.float32)


def narrow(x):
    return x.astype(jnp.bfloat16)


def pick(x, k, dim):
    return lax.dynamic_index_in_dim(x, k, dim, keepdims=False)


def turn(x, axis, step):
    n = lax.axis_size(axis)
    return lax.ppermute(x, axis, [(k, (k + step) % n) for k in range(n)])


def x_sum(own, m):
    parts = [turn(pick(own, (m + s) % 4, 1), "rep_1", s) for s in (2, 1, 3)]
    total = wide(pick(own, m, 1))
    for part in parts:
        total = total + wide(part)
    return total


def x_gather(rows, m):
    out = jnp.zeros((rows.shape[0], 4, *rows.shape[1:]), rows.dtype)
    parts = [(turn(rows, "rep_1", s), (m - s) % 4) for s in (2, 1, 3)]
    for part, k in [(rows, m), *parts[1:], parts[0]]:
        out = lax.dynamic_update_slice(out, part[:, None], (0, k, 0, 0))
    return out


def shards(deltas, pod_momentum, global_momentum, master):
    m, q = lax.axis_index("rep_1"), lax.axis_index("rep_0")
    pods = lax.axis_size("outer")
    n0 = lax.axis_size("rep_0")
    replicas = n0 * lax.axis_size("rep_1")
    columns = deltas.shape[-1]
    own = deltas[0, 0].reshape(n0, 4, -1, columns)
    total = x_sum(own, m)
    mine = jnp.arange(n0)[:, None, None] == q
    update = (1.9 / replicas) * total + jnp.where(mine, 0.81 * pod_momentum, 0.0)
    blocks = narrow(update).reshape(n0 * pods, -1, columns)
    blocks = lax.all_to_all(blocks, ZY, 0, 0, tiled=True)
    glob_mean = jnp.sum(wide(blocks), axis=0) / pods
    glob_new = 0.8 * global_momentum[0] + glob_mean
    fresh = narrow(master[0] - 0.7 * (glob_mean + 0.8 * glob_new))
    copies = jnp.broadcast_to(fresh[None], (n0 * pods, *fresh.shape))
    rows = lax.all_to_all(copies, ZY, 0, 0, tiled=True).reshape(n0, -1, columns)
    sent = [narrow(pick(total, (q + s) % n0, 0)) for s in (1, 2)]
    kept = pick(total, q, 0)
    rows, sent, kept = lax.optimization_barrier((rows, sent, kept))
    out = x_gather(rows, m)
    pod_total = kept
    for part, s in zip(sent, (1, 2), strict=True):
        pod_total = pod_total + wide(turn(part, "rep_0", s))
    pod_new = 0.9 * pod_momentum[0] + pod_total / replicas
    return (out.reshape(-1, columns), pod_new[None], glob_new[None])


def solution(mesh):
    finer = Mesh(
        mesh.devices.reshape(mesh.shape["outer"], 3, 4, mesh.shape["mp"]),
        ("outer", "rep_0", "rep_1", "mp"),
    )
    return jax.shard_map(
        shards,
        mesh=finer,
        in_specs=(
            P("outer", REP, None, "mp"),
            P("outer", REP, "mp"),
            P(REP, "outer", "mp"),
            P(REP, "outer", "mp"),
        ),
        out_specs=(P(None, "mp"), P("outer", REP, "mp"), P(REP, "outer", "mp")),
        check_vma=False,
    )
```

```python
import jax
import jax.numpy as jnp
from jax import lax
from jax.sharding import Mesh
from jax.sharding import PartitionSpec as P

REP = ("rep_0", "rep_1")


def wide(x):
    return x.astype(jnp.float32)


def narrow(x):
    return x.astype(jnp.bfloat16)


def pick(x, k, dim):
    return lax.dynamic_index_in_dim(x, k, dim, keepdims=False)


def turn(x, axis, step):
    n = lax.axis_size(axis)
    return lax.ppermute(x, axis, [(k, (k + step) % n) for k in range(n)])


def near(k):
    return k ^ 1


def far(k):
    return 3 - k


ROUTES = ((near, far), (far, near))


def hop(x, partner):
    return lax.ppermute(x, "rep_1", [(k, partner(k)) for k in range(4)])


def block(own, k, h):
    n, _, rows, columns = own.shape
    half = rows // 2
    return lax.dynamic_slice(own, (0, k, h * half, 0), (n, 1, half, columns))[:, 0]


def x_sum(own, m):
    arrived = []
    for h, (one, two) in enumerate(ROUTES):
        sent = [block(own, k, h) for k in (one(m), two(one(m)))]
        arrived.append(hop(jnp.stack(sent), one))
    lasts = []
    for h, (_, two) in enumerate(ROUTES):
        onward = wide(block(own, two(m), h)) + wide(arrived[h][1])
        lasts.append(hop(narrow(onward), two))
    parts = []
    for h in range(2):
        kept = wide(block(own, m, h)) + wide(arrived[h][0])
        parts.append(kept + wide(lasts[h]))
    return jnp.concatenate(parts, axis=1)


def x_gather(rows, m):
    pods, n, depth, columns = rows.shape
    half = pods // 2
    beside, across = hop(rows, near), hop(rows, far)
    front = hop(across[:half], near)
    back = hop(beside[half:], far)
    out = jnp.zeros((n, 4, pods * depth, columns), rows.dtype)
    pieces = (
        (rows, m, 0),
        (beside, near(m), 0),
        (across, far(m), 0),
        (front, near(far(m)), 0),
        (back, near(far(m)), half * depth),
    )
    for piece, k, row in pieces:
        piece = piece.swapaxes(0, 1).reshape(n, 1, -1, columns)
        out = lax.dynamic_update_slice(out, piece, (0, k, row, 0))
    return out


def z_all(x, q):
    n = lax.axis_size("rep_0")
    seen = jnp.stack([x, *(turn(x, "rep_0", s) for s in range(1, n))])
    return [pick(seen, (q - k) % n, 0) for k in range(n)]


def shards(deltas, pod_momentum, global_momentum, master):
    m, q = lax.axis_index("rep_1"), lax.axis_index("rep_0")
    pods = lax.axis_size("outer")
    n0 = lax.axis_size("rep_0")
    replicas = n0 * lax.axis_size("rep_1")
    columns = deltas.shape[-1]
    own = deltas[0, 0].reshape(n0, 4, -1, columns)
    rest = jnp.stack(z_all(master[0] - 0.448 * global_momentum[0], q))
    total = x_sum(own, m)
    mine = jnp.arange(n0)[:, None, None] == q
    update = (1.9 / replicas) * total + jnp.where(mine, 0.81 * pod_momentum, 0.0)
    blocks = narrow(update).reshape(n0, pods, -1, columns).swapaxes(0, 1)
    blocks = lax.all_to_all(blocks, "outer", 0, 0, tiled=True)
    by_z = z_all(narrow(jnp.sum(wide(blocks), axis=0)), q)
    glob_mean = sum(wide(part) for part in by_z) / pods
    fresh = narrow(rest - 1.26 * glob_mean)
    glob_new = 0.8 * global_momentum[0] + pick(glob_mean, q, 0)
    sent = [narrow(pick(total, (q + s) % n0, 0)) for s in (1, 2)]
    kept = pick(total, q, 0)
    fresh, sent, kept = lax.optimization_barrier((fresh, sent, kept))
    copies = jnp.broadcast_to(fresh[None], (pods, *fresh.shape))
    rows = lax.all_to_all(copies, "outer", 0, 0, tiled=True)
    out = x_gather(rows, m)
    pod_total = kept
    for part, s in zip(sent, (1, 2), strict=True):
        pod_total = pod_total + wide(turn(part, "rep_0", s))
    pod_new = 0.9 * pod_momentum[0] + pod_total / replicas
    return (out.reshape(-1, columns), pod_new[None], glob_new[None])


def solution(mesh):
    finer = Mesh(
        mesh.devices.reshape(mesh.shape["outer"], 3, 4, mesh.shape["mp"]),
        ("outer", "rep_0", "rep_1", "mp"),
    )
    return jax.shard_map(
        shards,
        mesh=finer,
        in_specs=(
            P("outer", REP, None, "mp"),
            P("outer", REP, "mp"),
            P(REP, "outer", "mp"),
            P(REP, "outer", "mp"),
        ),
        out_specs=(P(None, "mp"), P("outer", REP, "mp"), P(REP, "outer", "mp")),
        check_vma=False,
    )
```

```python
import jax
import jax.numpy as jnp
from jax import lax
from jax.sharding import Mesh
from jax.sharding import PartitionSpec as P

REP = ("rep_0", "rep_1")


def wide(x):
    return x.astype(jnp.float32)


def narrow(x):
    return x.astype(jnp.bfloat16)


def pick(x, k, dim):
    return lax.dynamic_index_in_dim(x, k, dim, keepdims=False)


def turn(x, axis, step):
    n = lax.axis_size(axis)
    return lax.ppermute(x, axis, [(k, (k + step) % n) for k in range(n)])


def block(own, k, h):
    n, _, rows, columns = own.shape
    half = rows // 2
    return lax.dynamic_slice(own, (0, k, h * half, 0), (n, 1, half, columns))[:, 0]


def x_sum(own, m):
    up, across, down = ((m + s) % 4 for s in (1, 2, 3))
    onward = turn(block(own, across, 0), "rep_1", 1)
    back = turn(block(own, across, 1), "rep_1", 3)
    from_down = turn(block(own, up, 1), "rep_1", 1)
    from_up = turn(block(own, down, 0), "rep_1", 3)
    onward, back = lax.optimization_barrier((onward, back))
    onward = turn(narrow(wide(block(own, up, 0)) + wide(onward)), "rep_1", 1)
    back = turn(narrow(wide(block(own, down, 1)) + wide(back)), "rep_1", 3)
    parts = (from_down, from_up, onward, back)
    from_down, from_up, onward, back = lax.optimization_barrier(parts)
    first = wide(block(own, m, 0)) + wide(from_up) + wide(onward)
    second = wide(block(own, m, 1)) + wide(from_down) + wide(back)
    return jnp.concatenate((first, second), axis=1)


def x_gather(rows, m):
    pods, n, depth, columns = rows.shape
    half = pods // 2
    first, second = (
        part.swapaxes(0, 1).reshape(n, half * depth, columns)
        for part in (rows[:half], rows[half:])
    )
    up, across, down = ((m + s) % 4 for s in (1, 2, 3))
    down_first = turn(first, "rep_1", 1)
    up_second = turn(second, "rep_1", 3)
    down_second = turn(second, "rep_1", 1)
    up_first = turn(first, "rep_1", 3)
    across_first = turn(down_first, "rep_1", 1)
    across_second = turn(up_second, "rep_1", 3)
    out = jnp.zeros((n, 4, pods * depth, columns), rows.dtype)
    pieces = (
        (first, m, 0),
        (second, m, half * depth),
        (down_first, down, 0),
        (up_second, up, half * depth),
        (down_second, down, half * depth),
        (up_first, up, 0),
        (across_first, across, 0),
        (across_second, across, half * depth),
    )
    for piece, k, row in pieces:
        out = lax.dynamic_update_slice(out, piece[:, None], (0, k, row, 0))
    return out, across_first


def z_all(x, q):
    n = lax.axis_size("rep_0")
    seen = jnp.stack([x, *(turn(x, "rep_0", s) for s in range(1, n))])
    return [pick(seen, (q - k) % n, 0) for k in range(n)]


def shards(deltas, pod_momentum, global_momentum, master):
    m, q = lax.axis_index("rep_1"), lax.axis_index("rep_0")
    pods = lax.axis_size("outer")
    n0 = lax.axis_size("rep_0")
    replicas = n0 * lax.axis_size("rep_1")
    columns = deltas.shape[-1]
    own = deltas[0, 0].reshape(n0, 4, -1, columns)
    rest = jnp.stack(z_all(master[0] - 0.448 * global_momentum[0], q))
    total = x_sum(own, m)
    mine = jnp.arange(n0)[:, None, None] == q
    update = (1.9 / replicas) * total + jnp.where(mine, 0.81 * pod_momentum, 0.0)
    blocks = narrow(update).reshape(n0, pods, -1, columns).swapaxes(0, 1)
    blocks = lax.all_to_all(blocks, "outer", 0, 0, tiled=True)
    by_z = z_all(narrow(jnp.sum(wide(blocks), axis=0)), q)
    glob_mean = sum(wide(part) for part in by_z) / pods
    fresh = narrow(rest - 1.26 * glob_mean)
    glob_new = 0.8 * global_momentum[0] + pick(glob_mean, q, 0)
    sent = [narrow(pick(total, (q + s) % n0, 0)) for s in (1, 2)]
    kept = pick(total, q, 0)
    fresh, sent, kept = lax.optimization_barrier((fresh, sent, kept))
    copies = jnp.broadcast_to(fresh[None], (pods, *fresh.shape))
    rows = lax.all_to_all(copies, "outer", 0, 0, tiled=True)
    others = [turn(part, "rep_0", s) for part, s in zip(sent, (1, 2), strict=True)]
    out, late = x_gather(rows, m)
    others, _ = lax.optimization_barrier((others, late))
    pod_total = kept + sum(wide(part) for part in others)
    pod_new = 0.9 * pod_momentum[0] + pod_total / replicas
    return (out.reshape(-1, columns), pod_new[None], glob_new[None])


def solution(mesh):
    finer = Mesh(
        mesh.devices.reshape(mesh.shape["outer"], 3, 4, mesh.shape["mp"]),
        ("outer", "rep_0", "rep_1", "mp"),
    )
    return jax.shard_map(
        shards,
        mesh=finer,
        in_specs=(
            P("outer", REP, None, "mp"),
            P("outer", REP, "mp"),
            P(REP, "outer", "mp"),
            P(REP, "outer", "mp"),
        ),
        out_specs=(P(None, "mp"), P("outer", REP, "mp"), P(REP, "outer", "mp")),
        check_vma=False,
    )
```

```python
import jax
import jax.numpy as jnp
from jax import lax
from jax.sharding import Mesh
from jax.sharding import PartitionSpec as P


REP = ("rep_0", "rep_1")


def wide(x):
    return x.astype(jnp.float32)


def narrow(x):
    return x.astype(jnp.bfloat16)


def pick(x, k, dim):
    return lax.dynamic_index_in_dim(x, k, dim, keepdims=False)


def turn(x, axis, step):
    n = lax.axis_size(axis)
    return lax.ppermute(x, axis, [(k, (k + step) % n) for k in range(n)])


def block(own, k, h):
    n, _, rows, columns = own.shape
    half = rows // 2
    return lax.dynamic_slice(own, (0, k, h * half, 0), (n, 1, half, columns))[:, 0]


def tagged(x, step):
    return turn(x, "rep_1", step)


def x_sum(own, m):
    up, across, down = ((m + s) % 4 for s in (1, 2, 3))
    ends = block(own, across, 0), block(own, across, 1)
    own, *ends = lax.optimization_barrier((own, *ends))
    onward = tagged(ends[0], 1)
    back = tagged(ends[1], 3)
    from_down = tagged(block(own, up, 1), 1)
    from_up = tagged(block(own, down, 0), 3)
    onward, back = lax.optimization_barrier((onward, back))
    onward = tagged(narrow(wide(block(own, up, 0)) + wide(onward)), 1)
    back = tagged(narrow(wide(block(own, down, 1)) + wide(back)), 3)
    parts = (from_down, from_up, onward, back)
    from_down, from_up, onward, back = lax.optimization_barrier(parts)
    first = wide(block(own, m, 0)) + wide(from_up) + wide(onward)
    second = wide(block(own, m, 1)) + wide(from_down) + wide(back)
    return jnp.concatenate((first, second), axis=1)


def x_gather(rows, m):
    pods, n, depth, columns = rows.shape
    half = pods // 2
    first, second = (
        part.swapaxes(0, 1).reshape(n, half * depth, columns)
        for part in (rows[:half], rows[half:])
    )
    up, across, down = ((m + s) % 4 for s in (1, 2, 3))
    down_first = tagged(first, 1)
    up_second = tagged(second, 3)
    down_second = tagged(second, 1)
    up_first = tagged(first, 3)
    across_first = tagged(down_first, 1)
    across_second = tagged(up_second, 3)
    out = jnp.zeros((n, 4, pods * depth, columns), rows.dtype)
    pieces = (
        (first, m, 0),
        (second, m, half * depth),
        (down_first, down, 0),
        (up_second, up, half * depth),
        (down_second, down, half * depth),
        (up_first, up, 0),
        (across_first, across, 0),
        (across_second, across, half * depth),
    )
    for piece, k, row in pieces:
        out = lax.dynamic_update_slice(out, piece[:, None], (0, k, row, 0))
    return out, across_first


def z_all(x, q):
    n = lax.axis_size("rep_0")
    seen = jnp.stack([x, *(turn(x, "rep_0", s) for s in range(1, n))])
    return [pick(seen, (q - k) % n, 0) for k in range(n)]


def step(deltas, pod_momentum, global_momentum, master):
    m, q = lax.axis_index("rep_1"), lax.axis_index("rep_0")
    pods = lax.axis_size("outer")
    n0 = lax.axis_size("rep_0")
    replicas = n0 * lax.axis_size("rep_1")
    columns = deltas.shape[-1]
    own = deltas[0, 0].reshape(n0, 4, -1, columns)
    rest = jnp.stack(z_all(master[0] - 0.448 * global_momentum[0], q))
    total = x_sum(own, m)
    mine = jnp.arange(n0)[:, None, None] == q
    update = (1.9 / replicas) * total + jnp.where(mine, 0.81 * pod_momentum, 0.0)
    blocks = narrow(update).reshape(n0, pods, -1, columns).swapaxes(0, 1)
    blocks = lax.all_to_all(blocks, "outer", 0, 0, tiled=True)
    by_z = z_all(narrow(jnp.sum(wide(blocks), axis=0)), q)
    glob_mean = sum(wide(part) for part in by_z) / pods
    fresh = narrow(rest - 1.26 * glob_mean)
    glob_new = 0.8 * global_momentum[0] + pick(glob_mean, q, 0)
    sent = [narrow(pick(total, (q + s) % n0, 0)) for s in (1, 2)]
    kept = pick(total, q, 0)
    fresh, sent, kept = lax.optimization_barrier((fresh, sent, kept))
    copies = jnp.broadcast_to(fresh[None], (pods, *fresh.shape))
    rows = lax.all_to_all(copies, "outer", 0, 0, tiled=True)
    others = [turn(part, "rep_0", s) for part, s in zip(sent, (1, 2), strict=True)]
    out, late = x_gather(rows, m)
    others, _ = lax.optimization_barrier((others, late))
    pod_total = kept + sum(wide(part) for part in others)
    pod_new = 0.9 * pod_momentum[0] + pod_total / replicas
    return (out.reshape(-1, columns), pod_new[None], glob_new[None])


def solution(mesh):
    finer = Mesh(
        mesh.devices.reshape(mesh.shape["outer"], 3, 4, mesh.shape["mp"]),
        ("outer", "rep_0", "rep_1", "mp"),
    )
    return jax.shard_map(
        step,
        mesh=finer,
        in_specs=(
            P("outer", REP, None, "mp"),
            P("outer", REP, "mp"),
            P(REP, "outer", "mp"),
            P(REP, "outer", "mp"),
        ),
        out_specs=(P(None, "mp"), P("outer", REP, "mp"), P(REP, "outer", "mp")),
        check_vma=False,
    )
```

```python
import jax
import jax.numpy as jnp
from jax import lax
from jax.sharding import Mesh
from jax.sharding import PartitionSpec as P


REP = ("rep_0", "rep_1")


def wide(x):
    return x.astype(jnp.float32)


def narrow(x):
    return x.astype(jnp.bfloat16)


def pick(x, k, dim):
    return lax.dynamic_index_in_dim(x, k, dim, keepdims=False)


def sign(core):
    return 1 - 2 * (core % 2)


def place(k, axis, step):
    n = lax.axis_size(axis)
    return (k + n + sign(lax.axis_index("mp")) * step) % n


def turn(x, axis, step):
    n, width = lax.axis_size(axis), lax.axis_size("mp")
    pairs = [
        (k * width + c, (k + sign(c) * step) % n * width + c)
        for k in range(n)
        for c in range(width)
    ]
    return lax.ppermute(x, (axis, "mp"), pairs)


def block(own, k, h):
    n, _, rows, columns = own.shape
    half = rows // 2
    return lax.dynamic_slice(own, (0, k, h * half, 0), (n, 1, half, columns))[:, 0]


def tagged(x, step):
    return turn(x, "rep_1", step)


def x_sum(own, m):
    up, across, down = (place(m, "rep_1", s) for s in (1, 2, 3))
    ends = block(own, across, 0), block(own, across, 1)
    own, *ends = lax.optimization_barrier((own, *ends))
    onward = tagged(ends[0], 1)
    back = tagged(ends[1], 3)
    from_down = tagged(block(own, up, 1), 1)
    from_up = tagged(block(own, down, 0), 3)
    onward, back = lax.optimization_barrier((onward, back))
    onward = tagged(narrow(wide(block(own, up, 0)) + wide(onward)), 1)
    back = tagged(narrow(wide(block(own, down, 1)) + wide(back)), 3)
    parts = (from_down, from_up, onward, back)
    from_down, from_up, onward, back = lax.optimization_barrier(parts)
    first = wide(block(own, m, 0)) + wide(from_up) + wide(onward)
    second = wide(block(own, m, 1)) + wide(from_down) + wide(back)
    return jnp.concatenate((first, second), axis=1)


def x_gather(rows, m):
    pods, n, depth, columns = rows.shape
    half = pods // 2
    first, second = (
        part.swapaxes(0, 1).reshape(n, half * depth, columns)
        for part in (rows[:half], rows[half:])
    )
    up, across, down = (place(m, "rep_1", s) for s in (1, 2, 3))
    down_first = tagged(first, 1)
    up_second = tagged(second, 3)
    down_second = tagged(second, 1)
    up_first = tagged(first, 3)
    across_first = tagged(down_first, 1)
    across_second = tagged(up_second, 3)
    out = jnp.zeros((n, 4, pods * depth, columns), rows.dtype)
    pieces = (
        (first, m, 0),
        (second, m, half * depth),
        (down_first, down, 0),
        (up_second, up, half * depth),
        (down_second, down, half * depth),
        (up_first, up, 0),
        (across_first, across, 0),
        (across_second, across, half * depth),
    )
    for piece, k, row in pieces:
        out = lax.dynamic_update_slice(out, piece[:, None], (0, k, row, 0))
    return out, across_first


def z_all(x, q):
    n = lax.axis_size("rep_0")
    seen = jnp.stack([x, *(turn(x, "rep_0", s) for s in range(1, n))])
    away = sign(lax.axis_index("mp"))
    return [pick(seen, (n + away * (q - k)) % n, 0) for k in range(n)]


def step(deltas, pod_momentum, global_momentum, master):
    m, q = lax.axis_index("rep_1"), lax.axis_index("rep_0")
    pods = lax.axis_size("outer")
    n0 = lax.axis_size("rep_0")
    replicas = n0 * lax.axis_size("rep_1")
    columns = deltas.shape[-1]
    own = deltas[0, 0].reshape(n0, 4, -1, columns)
    rest = jnp.stack(z_all(master[0] - 0.448 * global_momentum[0], q))
    total = x_sum(own, m)
    mine = jnp.arange(n0)[:, None, None] == q
    update = (1.9 / replicas) * total + jnp.where(mine, 0.81 * pod_momentum, 0.0)
    blocks = narrow(update).reshape(n0, pods, -1, columns).swapaxes(0, 1)
    blocks = lax.all_to_all(blocks, "outer", 0, 0, tiled=True)
    by_z = z_all(narrow(jnp.sum(wide(blocks), axis=0)), q)
    glob_mean = sum(wide(part) for part in by_z) / pods
    fresh = narrow(rest - 1.26 * glob_mean)
    glob_new = 0.8 * global_momentum[0] + pick(glob_mean, q, 0)
    sent = [narrow(pick(total, place(q, "rep_0", s), 0)) for s in (1, 2)]
    kept = pick(total, q, 0)
    fresh, sent, kept = lax.optimization_barrier((fresh, sent, kept))
    copies = jnp.broadcast_to(fresh[None], (pods, *fresh.shape))
    rows = lax.all_to_all(copies, "outer", 0, 0, tiled=True)
    others = [turn(part, "rep_0", s) for part, s in zip(sent, (1, 2), strict=True)]
    out, late = x_gather(rows, m)
    others, _ = lax.optimization_barrier((others, late))
    pod_total = kept + sum(wide(part) for part in others)
    pod_new = 0.9 * pod_momentum[0] + pod_total / replicas
    return (out.reshape(-1, columns), pod_new[None], glob_new[None])


def solution(mesh):
    finer = Mesh(
        mesh.devices.reshape(mesh.shape["outer"], 3, 4, mesh.shape["mp"]),
        ("outer", "rep_0", "rep_1", "mp"),
    )
    return jax.shard_map(
        step,
        mesh=finer,
        in_specs=(
            P("outer", REP, None, "mp"),
            P("outer", REP, "mp"),
            P(REP, "outer", "mp"),
            P(REP, "outer", "mp"),
        ),
        out_specs=(P(None, "mp"), P("outer", REP, "mp"), P(REP, "outer", "mp")),
        check_vma=False,
    )
```

```python
import jax
import jax.numpy as jnp
from jax import lax
from jax.sharding import Mesh
from jax.sharding import PartitionSpec as P


REP = ("rep_0", "rep_1")


def wide(x):
    return x.astype(jnp.float32)


def narrow(x):
    return x.astype(jnp.bfloat16)


def pick(x, k, dim):
    return lax.dynamic_index_in_dim(x, k, dim, keepdims=False)


def turn(x, axis, step):
    n = lax.axis_size(axis)
    return lax.ppermute(x, axis, [(k, (k + step) % n) for k in range(n)])


def block(own, k, h):
    n, _, rows, columns = own.shape
    half = rows // 2
    return lax.dynamic_slice(own, (0, k, h * half, 0), (n, 1, half, columns))[:, 0]


def tagged(x, step):
    return turn(x, "rep_1", step)


def x_sum(own, m):
    up, across, down = ((m + s) % 4 for s in (1, 2, 3))
    ends = block(own, across, 0), block(own, across, 1)
    own, *ends = lax.optimization_barrier((own, *ends))
    onward = tagged(ends[0], 1)
    back = tagged(ends[1], 3)
    from_down = tagged(block(own, up, 1), 1)
    from_up = tagged(block(own, down, 0), 3)
    onward, back = lax.optimization_barrier((onward, back))
    onward = tagged(narrow(wide(block(own, up, 0)) + wide(onward)), 1)
    back = tagged(narrow(wide(block(own, down, 1)) + wide(back)), 3)
    parts = (own, from_down, from_up, onward)
    own, from_down, from_up, onward = lax.optimization_barrier(parts)
    first = wide(block(own, m, 0)) + wide(from_up) + wide(onward)
    second = wide(block(own, m, 1)) + wide(from_down)
    first, second, back = lax.optimization_barrier((first, second, back))
    return jnp.concatenate((first, second + wide(back)), axis=1)


def x_gather(rows, m):
    pods, n, depth, columns = rows.shape
    half = pods // 2
    first, second = (
        part.swapaxes(0, 1).reshape(n, half * depth, columns)
        for part in (rows[:half], rows[half:])
    )
    up, across, down = ((m + s) % 4 for s in (1, 2, 3))
    down_first = tagged(first, 1)
    up_second = tagged(second, 3)
    down_second = tagged(second, 1)
    up_first = tagged(first, 3)
    across_first = tagged(down_first, 1)
    across_second = tagged(up_second, 3)
    out = jnp.zeros((n, 4, pods * depth, columns), rows.dtype)
    pieces = (
        (first, m, 0),
        (second, m, half * depth),
        (down_first, down, 0),
        (up_second, up, half * depth),
        (down_second, down, half * depth),
        (up_first, up, 0),
        (across_first, across, 0),
        (across_second, across, half * depth),
    )
    for piece, k, row in pieces:
        out = lax.dynamic_update_slice(out, piece[:, None], (0, k, row, 0))
    return out, across_first


def z_all(x, q):
    n = lax.axis_size("rep_0")
    seen = jnp.stack([x, *(turn(x, "rep_0", s) for s in range(1, n))])
    return [pick(seen, (q - k) % n, 0) for k in range(n)]


def step(deltas, pod_momentum, global_momentum, master):
    m, q = lax.axis_index("rep_1"), lax.axis_index("rep_0")
    pods = lax.axis_size("outer")
    n0 = lax.axis_size("rep_0")
    replicas = n0 * lax.axis_size("rep_1")
    columns = deltas.shape[-1]
    own = deltas[0, 0].reshape(n0, 4, -1, columns)
    rest = jnp.stack(z_all(master[0] - 0.448 * global_momentum[0], q))
    total = x_sum(own, m)
    mine = jnp.arange(n0)[:, None, None] == q
    update = (1.9 / replicas) * total + jnp.where(mine, 0.81 * pod_momentum, 0.0)
    blocks = narrow(update).reshape(n0, pods, -1, columns).swapaxes(0, 1)
    blocks = lax.all_to_all(blocks, "outer", 0, 0, tiled=True)
    by_z = z_all(narrow(jnp.sum(wide(blocks), axis=0)), q)
    glob_mean = sum(wide(part) for part in by_z) / pods
    fresh = narrow(rest - 1.26 * glob_mean)
    glob_new = 0.8 * global_momentum[0] + pick(glob_mean, q, 0)
    sent = [narrow(pick(total, (q + s) % n0, 0)) for s in (1, 2)]
    kept = pick(total, q, 0)
    fresh, sent, kept = lax.optimization_barrier((fresh, sent, kept))
    copies = jnp.broadcast_to(fresh[None], (pods, *fresh.shape))
    rows = lax.all_to_all(copies, "outer", 0, 0, tiled=True)
    others = [turn(part, "rep_0", s) for part, s in zip(sent, (1, 2), strict=True)]
    out, late = x_gather(rows, m)
    others, _ = lax.optimization_barrier((others, late))
    pod_total = kept + sum(wide(part) for part in others)
    pod_new = 0.9 * pod_momentum[0] + pod_total / replicas
    return (out.reshape(-1, columns), pod_new[None], glob_new[None])


def solution(mesh):
    finer = Mesh(
        mesh.devices.reshape(mesh.shape["outer"], 3, 4, mesh.shape["mp"]),
        ("outer", "rep_0", "rep_1", "mp"),
    )
    return jax.shard_map(
        step,
        mesh=finer,
        in_specs=(
            P("outer", REP, None, "mp"),
            P("outer", REP, "mp"),
            P(REP, "outer", "mp"),
            P(REP, "outer", "mp"),
        ),
        out_specs=(P(None, "mp"), P("outer", REP, "mp"), P(REP, "outer", "mp")),
        check_vma=False,
    )
```
